256 devices in a mesh: gy: 4 (over z_hi), gx: 64 (over y, x, z_lo, core).
Axes of the slice: x: 4, y: 4, z: 8 (z_hi: 4, z_lo: 2; z = z_hi * 2 + z_lo), core: 2. Of those that a mesh axis runs over, the one named last changes fastest.
Arguments:
- inputs: bfloat16 [128, 4096, 256], P('gy', 'gx'), may hold values from -6 to 6
- cotangent: bfloat16 [128, 4096, 256], P('gy', 'gx'), may hold values from -6 to 6
- mode_weight: bfloat16 [2, 32, 256, 256], P(None, None, 'gx'), may hold values from -2.09375 to 2.09375
- w_in: bfloat16 [256, 1024], replicated, may hold values from -0.375 to 0.375
- w_out: bfloat16 [1024, 256], replicated, may hold values from -0.1875 to 0.1875
Outputs:
- d_inputs: bfloat16 [128, 4096, 256], P('gy', 'gx')
- d_mode: float32 [2, 32, 256, 256], P(None, 'gy', 'gx')
- d_w_in: float32 [256, 1024], P(None, ('gy', 'gx'))
- d_w_out: float32 [1024, 256], P(('gy', 'gx'))
The draws below stay inside these ranges and needn't reach their ends.
All inputs are finite; a program needn't handle non-finite values.
Results may differ from the reference program's by a relative error of at most 0.014.
Values may be sent and summed in bfloat16 or wider, within the bound.
No kernel may reach another device: no remote copies, remote signals or barrier semaphores. Data moves between devices by JAX's collectives and lax.ppermute only.
A program may use at most 64 MiB of HBM per device.

```python
import math
import jax
import jax.numpy as jnp
from jax import lax

C = 256
H = 1024
M = 32
LINES = 128
NX = 4096


def level_of(rng, dims, shards, smallest, top_value):
    gain, own = 1.0, jax.random.fold_in(rng, 6)
    for position, blocks in shards:
        heights = jnp.exp(jax.random.uniform(jax.random.fold_in(own, position), (blocks,), jnp.float32, smallest / len(shards), top_value / len(shards)))
        gain = gain * jnp.repeat(heights, dims[position] // blocks).reshape([-1 if axis == position else 1 for axis in range(len(dims))])
    return gain


def normal_values(stream_key, dims, scale, reach, pieces=(), kind=jnp.bfloat16):
    array = jax.random.normal(stream_key, dims, jnp.float32) * scale
    if len(pieces) > 0:
        array = level_of(stream_key, dims, pieces, -0.22, 0.18) * array
    return jnp.clip(array, min=-reach, max=reach).astype(kind)


def setup_inputs(seed: int = 0) -> dict:
    key_of = jax.random.split(jax.random.key(seed), 6)
    inputs = normal_values(key_of[0], (LINES, NX, C), 1.0, 6.0, ((0, 4), (1, 64)))
    cotangent = normal_values(key_of[1], (LINES, NX, C), 1.0, 6.0, ((0, 4), (1, 64)))
    mode_weight = normal_values(key_of[2], (2, M, C, C), 0.35, 2.09375, ((2, 64),))
    w_in = normal_values(key_of[3], (C, H), C ** -0.5, 0.375)
    w_out = normal_values(key_of[4], (H, C), H ** -0.5, 0.1875)
    return dict(inputs=inputs, cotangent=cotangent, mode_weight=mode_weight, w_in=w_in, w_out=w_out)


def bases(positions, length, modes):
    order = jnp.arange(modes, dtype=jnp.int32)
    phase = positions[:, None] * order[None, :] % length
    angle = phase.astype(jnp.float32) * (2.0 * math.pi / length)
    factor = 1.0 / math.sqrt(length)
    cosine = jnp.cos(angle) * factor
    sine = jnp.sin(angle) * factor
    forward = jnp.concatenate([cosine, -sine], axis=1).astype(jnp.bfloat16)
    weight = jnp.where(order == 0, 1.0, 2.0).astype(jnp.float32)
    inverse = jnp.concatenate([cosine * weight, -sine * weight], axis=1).T.astype(jnp.bfloat16)
    return (forward, inverse)

def smooth_gate(values):
    return jax.nn.gelu(values, approximate=True)

def contract(form, left, right):
    return jnp.einsum(form, left.astype(jnp.float32), right.astype(jnp.float32))

def reference(inputs, cotangent, mode_weight, w_in, w_out):
    block = math.gcd(LINES, 8)
    nblocks = LINES // block
    positions = jnp.arange(NX, dtype=jnp.int32)
    forward, inverse = bases(positions, NX, M)
    w_re = mode_weight[0]
    w_im = mode_weight[1]
    in_blocks = inputs.reshape(nblocks, block, NX, C)
    cot_blocks = cotangent.reshape(nblocks, block, NX, C)

    def step(carry, pair):
        acc_in, acc_out, acc_mode = carry
        field, grad = pair
        spectrum = contract('yxc,xm->cmy', field, forward).astype(jnp.bfloat16)
        own_re = spectrum[:, :M]
        own_im = spectrum[:, M:]
        vr = contract('cky,kco->oky', own_re, w_re) - contract('cky,kco->oky', own_im, w_im)
        vi = contract('cky,kco->oky', own_re, w_im) + contract('cky,kco->oky', own_im, w_re)
        mixed = jnp.concatenate([vr, vi], axis=1).astype(jnp.bfloat16)
        hidden = contract('omy,mx->yxo', mixed, inverse).astype(jnp.bfloat16)
        flat_h = hidden.reshape(-1, C)
        flat_g = grad.reshape(-1, C)
        pre = jnp.dot(flat_h, w_in, preferred_element_type=jnp.float32)
        act, pullback = jax.vjp(smooth_gate, pre)
        act = act.astype(jnp.bfloat16)
        acc_out = acc_out + jnp.dot(act.T, flat_g, preferred_element_type=jnp.float32)
        grad_act = jnp.dot(flat_g, w_out.T, preferred_element_type=jnp.float32)
        d_pre = pullback(grad_act)[0].astype(jnp.bfloat16)
        acc_in = acc_in + jnp.dot(flat_h.T, d_pre, preferred_element_type=jnp.float32)
        d_hidden = jnp.dot(d_pre, w_in.T, preferred_element_type=jnp.float32).astype(jnp.bfloat16)
        d_hidden = d_hidden.reshape(block, NX, C)
        d_mixed = contract('yxo,mx->omy', d_hidden, inverse).astype(jnp.bfloat16)
        dv_re = d_mixed[:, :M]
        dv_im = d_mixed[:, M:]
        g_re = contract('cky,oky->kco', own_re, dv_re) + contract('cky,oky->kco', own_im, dv_im)
        g_im = contract('cky,oky->kco', own_re, dv_im) - contract('cky,oky->kco', own_im, dv_re)
        acc_mode = acc_mode + jnp.stack([g_re, g_im], axis=0)
        du_re = contract('kco,oky->cky', w_re, dv_re) + contract('kco,oky->cky', w_im, dv_im)
        du_im = contract('kco,oky->cky', w_re, dv_im) - contract('kco,oky->cky', w_im, dv_re)
        d_spectrum = jnp.concatenate([du_re, du_im], axis=1).astype(jnp.bfloat16)
        result = grad.astype(jnp.float32) + contract('cmy,xm->yxc', d_spectrum, forward)
        return ((acc_in, acc_out, acc_mode), result.astype(jnp.bfloat16))
    start = (jnp.zeros((C, H), jnp.float32), jnp.zeros((H, C), jnp.float32), jnp.zeros((2, M, C, C), jnp.float32))
    (acc_in, acc_out, acc_mode), results = lax.scan(step, start, (in_blocks, cot_blocks))
    scale_mlp = 1.0 / math.sqrt(LINES * NX)
    scale_mode = 1.0 / math.sqrt(LINES)
    d_inputs = results.reshape(LINES, NX, C)
    return (d_inputs, acc_mode * scale_mode, acc_in * scale_mlp, acc_out * scale_mlp)
```

```python
import math

import jax
import jax.numpy as jnp
from jax import lax
from jax.sharding import PartitionSpec as P

M = 32
BF = jnp.bfloat16
F32 = jnp.float32


def bases(positions, length, modes):
    order = jnp.arange(modes, dtype=jnp.int32)
    phase = positions[:, None] * order[None, :] % length
    angle = phase.astype(F32) * (2.0 * math.pi / length)
    factor = 1.0 / math.sqrt(length)
    cosine = jnp.cos(angle) * factor
    sine = jnp.sin(angle) * factor
    weight = jnp.where(order == 0, 1.0, 2.0).astype(F32)
    forward = jnp.stack([cosine, -sine], axis=2).astype(BF)
    inverse = jnp.stack([cosine * weight, -sine * weight], axis=2).astype(BF)
    size = positions.shape[0]
    return forward.reshape(size, 2 * modes), inverse.reshape(size, 2 * modes)


def smooth_gate(values):
    return jax.nn.gelu(values, approximate=True)


def contract(form, left, right):
    return jnp.einsum(form, left, right, preferred_element_type=F32)


def local(inputs, cotangent, mode_weight, w_in, w_out):
    lines, cols, chan = inputs.shape
    nx = lax.axis_size("gx")
    ny = lax.axis_size("gy")
    chips = nx // 2
    total_x = cols * nx
    half = lines // 2
    own_rows = chan // nx
    hid = w_in.shape[1]
    me = lax.axis_index("gx")
    core = me % 2
    groups = [[2 * t + c for t in range(chips)] for c in range(2)]
    swap = [(i, i ^ 1) for i in range(nx)]

    def pair(x):
        return lax.ppermute(x, "gx", swap)

    def spread(x):
        return lax.all_to_all(x, "gx", 0, 0, tiled=True, axis_index_groups=groups)

    def pick(x, which, axis):
        return lax.dynamic_index_in_dim(x, which, axis, keepdims=False)

    inp2 = inputs.reshape(2, half, cols, chan)
    cot2 = cotangent.reshape(2, half, cols, chan)
    in_par = pair(pick(inp2, 1 - core, 0))
    cot_par = pair(pick(cot2, 1 - core, 0))
    in_own = pick(inp2, core, 0)
    cot_own = pick(cot2, core, 0)
    steps = jnp.arange(cols, dtype=jnp.int32)
    own_fwd, own_inv = bases(me * cols + steps, total_x, M)
    par_fwd, par_inv = bases((me ^ 1) * cols + steps, total_x, M)
    inv = jnp.concatenate([own_inv, par_inv], axis=0)

    spec_part = contract("yxc,xm->myc", in_own, own_fwd) + contract("yxc,xm->myc", in_par, par_fwd)
    spec_part = spec_part.astype(BF).reshape(chips, 2 * half, chan)
    weight_rows = mode_weight.transpose(1, 0, 2, 3).reshape(M, 2 * own_rows, chan)
    recv = spread(jnp.concatenate([spec_part, weight_rows], axis=1))
    spec = recv[:, : 2 * half].astype(F32).sum(0).astype(BF).reshape(2, half, chan)
    w_mine = recv[:, 2 * half :].reshape(chips, 2, own_rows, chan)
    w_par = pair(w_mine)
    w_even = jnp.where(core == 0, w_mine, w_par)
    w_odd = jnp.where(core == 0, w_par, w_mine)
    w_all = jnp.stack([w_even, w_odd], axis=1).transpose(2, 0, 1, 3, 4).reshape(2, chan, chan)
    w_re, w_im = w_all[0], w_all[1]
    u_re, u_im = spec[0], spec[1]
    vr = contract("yc,co->yo", u_re, w_re) - contract("yc,co->yo", u_im, w_im)
    vi = contract("yc,co->yo", u_re, w_im) + contract("yc,co->yo", u_im, w_re)
    mixed = jnp.concatenate([vr, vi], axis=0).astype(BF)
    mixed = spread(jnp.broadcast_to(mixed[None], (chips, 2 * half, chan)))
    mixed = mixed.reshape(2 * M, half, chan)
    spec_par = pair(spec)

    hidden = contract("myo,xm->yxo", mixed, inv).astype(BF)
    flat_g = jnp.concatenate([cot_own, cot_par], axis=1).reshape(lines * cols, chan)
    flat_h = hidden.reshape(lines * cols, chan)
    pre = jnp.dot(flat_h, w_in, preferred_element_type=F32)
    act, pullback = jax.vjp(smooth_gate, pre)
    act = act.astype(BF)
    grad_out = contract("ph,pc->hc", act, flat_g)
    grad_act = contract("pc,hc->ph", flat_g, w_out)
    d_pre = pullback(grad_act)[0].astype(BF)
    grad_in = contract("ph,pc->hc", d_pre, flat_h)
    d_hidden = contract("ph,ch->pc", d_pre, w_in).astype(BF).reshape(half, 2 * cols, chan)
    d_part = contract("yxo,xm->myo", d_hidden, inv).astype(BF).reshape(chips, 2 * half, chan)
    grads = jnp.stack([grad_in, grad_out], axis=0)
    grads = grads.reshape(2, ny, chips, 2, hid // (ny * nx), chan)
    g_par = pair(pick(grads, 1 - core, 3).astype(BF))
    g_own = pick(grads, core, 3)

    dv = spread(d_part).astype(F32).sum(0).astype(BF).reshape(2, half, chan)
    dv_par = pair(dv)
    d_re, d_im = dv[0], dv[1]
    du_re = contract("yo,co->yc", d_re, w_re) + contract("yo,co->yc", d_im, w_im)
    du_im = contract("yo,co->yc", d_im, w_re) - contract("yo,co->yc", d_re, w_im)
    du = jnp.concatenate([du_re, du_im], axis=0).astype(BF)
    u_all = jnp.concatenate([spec, spec_par], axis=1)
    d_all = jnp.concatenate([dv, dv_par], axis=1)
    g_re = contract("yc,yo->co", u_all[0], d_all[0]) + contract("yc,yo->co", u_all[1], d_all[1])
    g_im = contract("yc,yo->co", u_all[0], d_all[1]) - contract("yc,yo->co", u_all[1], d_all[0])
    mode_rows = jnp.stack([g_re, g_im], axis=0).astype(BF).reshape(2, chips, 2, own_rows, chan)
    mode_rows = pick(mode_rows, core, 2).transpose(1, 0, 2, 3).reshape(chips, 2 * own_rows, chan)
    g_sum = (g_own + g_par.astype(F32)).astype(BF)
    g_rows = g_sum.transpose(2, 0, 1, 3, 4).reshape(chips, -1, chan)
    du_rows = jnp.broadcast_to(du[None], (chips, 2 * half, chan))
    recv = spread(jnp.concatenate([du_rows, mode_rows, g_rows], axis=1))
    a, b = 2 * half, 2 * half + 2 * own_rows
    du_own = recv[:, :a]
    du_par = pair(du_own)
    mode_part = recv[:, a:b].reshape(ny, M // ny, 2 * own_rows, chan)
    g_all = recv[:, b:].astype(F32).sum(0).reshape(2, ny, hid // (ny * nx), chan)
    g_all = g_all.transpose(1, 0, 2, 3).reshape(ny, -1, chan)
    gy = lax.axis_index("gy")
    blocks = jnp.concatenate([mode_part.reshape(ny, -1, chan), g_all.astype(BF)], axis=1)
    mode_sum = pick(mode_part, gy, 0).astype(F32).reshape(-1, chan)
    total = jnp.concatenate([mode_sum, pick(g_all, gy, 0)], axis=0)
    for d in range(1, ny):
        sent = pick(blocks, (gy + d) % ny, 0)
        total = total + lax.ppermute(sent, "gy", [(i, (i + d) % ny) for i in range(ny)]).astype(F32)
    cut = mode_sum.shape[0]
    d_mode = total[:cut].reshape(M // ny, 2, own_rows, chan).transpose(1, 0, 2, 3)
    tail = total[cut:].reshape(2, hid // (ny * nx), chan)

    du_lo = jnp.where(core == 0, du_own, du_par).reshape(2 * M, half, chan)
    du_hi = jnp.where(core == 0, du_par, du_own).reshape(2 * M, half, chan)
    ret_lo = contract("myc,xm->yxc", du_lo, own_fwd)
    ret_hi = contract("myc,xm->yxc", du_hi, own_fwd)
    returned = jnp.concatenate([ret_lo, ret_hi], axis=0)
    d_inputs = (cotangent.astype(F32) + returned).astype(BF)
    scale_mlp = 1.0 / math.sqrt(lines * ny * total_x)
    scale_mode = 1.0 / math.sqrt(lines * ny)
    return (d_inputs, d_mode * scale_mode, tail[0].T * scale_mlp, tail[1] * scale_mlp)


def solution(mesh):
    placed = (P("gy", "gx", None), P("gy", "gx", None), P(None, None, "gx", None), P(), P())
    return jax.shard_map(
        local,
        mesh=mesh,
        in_specs=placed,
        out_specs=(
            P("gy", "gx", None),
            P(None, "gy", "gx", None),
            P(None, ("gy", "gx")),
            P(("gy", "gx"), None),
        ),
        check_vma=False,
    )
```

```python
import math

import jax
import jax.numpy as jnp
from jax import lax
from jax.experimental import pallas as pl
from jax.experimental.pallas import tpu as pltpu
from jax.sharding import PartitionSpec as P

M = 32
LANES = 128
BF = jnp.bfloat16
F32 = jnp.float32


def bases(positions, length, modes):
    order = jnp.arange(modes, dtype=jnp.int32)
    phase = positions[:, None] * order[None, :] % length
    angle = phase.astype(F32) * (2.0 * math.pi / length)
    factor = 1.0 / math.sqrt(length)
    cosine = jnp.cos(angle) * factor
    sine = jnp.sin(angle) * factor
    weight = jnp.where(order == 0, 1.0, 2.0).astype(F32)
    forward = jnp.stack([cosine, -sine], axis=2).astype(BF)
    inverse = jnp.stack([cosine * weight, -sine * weight], axis=2).astype(BF)
    size = positions.shape[0]
    return forward.reshape(size, 2 * modes), inverse.reshape(size, 2 * modes)


def contract(form, left, right):
    return jnp.einsum(form, left, right, preferred_element_type=F32)


def dot(left, right):
    return jnp.dot(left, right, preferred_element_type=F32)


def rows_dot(left, right):
    return lax.dot_general(left, right, (((0,), (0,)), ((), ())), preferred_element_type=F32)


def grad_act_kernel(own_ref, par_ref, wt_ref, out_ref):
    block, cols, _ = own_ref.shape
    for y in range(block):
        base = 2 * cols * y
        out_ref[base : base + cols, :] = dot(own_ref[y], wt_ref[...])
        out_ref[base + cols : base + 2 * cols, :] = dot(par_ref[y], wt_ref[...])


def grad_act_call(own, par, w_out_t):
    half, cols, chan = own.shape
    hid = w_out_t.shape[1]
    block = 4
    return pl.pallas_call(
        grad_act_kernel,
        grid=(half // block,),
        in_specs=[
            pl.BlockSpec((block, cols, chan), lambda i: (i, 0, 0)),
            pl.BlockSpec((block, cols, chan), lambda i: (i, 0, 0)),
            pl.BlockSpec((chan, hid), lambda i: (0, 0)),
        ],
        out_specs=pl.BlockSpec((block * 2 * cols, hid), lambda i: (i, 0)),
        out_shape=jax.ShapeDtypeStruct((half * 2 * cols, hid), F32),
        name="grad_act",
    )(own, par, w_out_t)


GELU_A = math.sqrt(2.0 / math.pi)
GELU_B = 0.044715 * GELU_A


def mlp_kernel(mix_ref, ga_ref, inv_ref, invt_ref, wi_ref, wit_ref, hid_ref, act_ref, dpre_ref, part_ref, mix_lo, mix_hi, part_lo, part_hi):
    i = pl.program_id(0)
    rows, _ = hid_ref.shape
    cols = inv_ref.shape[0]
    block = rows // cols
    modes = inv_ref.shape[1]
    half = mix_ref.shape[0] // modes
    width = wi_ref.shape[1]
    piece = 256

    @pl.when(i == 0)
    def _():
        mix_lo[...] = mix_ref[:, :LANES].astype(F32)
        mix_hi[...] = mix_ref[:, LANES:].astype(F32)

    for b in range(block):
        lines = pl.ds(i * block + b, modes, stride=half)
        table = jnp.concatenate([mix_lo[lines, :], mix_hi[lines, :]], axis=1).astype(BF)
        hid_ref[b * cols : (b + 1) * cols, :] = dot(inv_ref[...], table).astype(BF)
    hidden = hid_ref[...]
    total = None
    for start in range(0, width, piece):
        sl = slice(start, start + piece)
        p = dot(hidden, wi_ref[:, sl])
        sq = p * p
        t = jnp.tanh(p * (GELU_A + GELU_B * sq))
        s = 0.5 + 0.5 * t
        act = p * s
        slope = s + act * (1.0 - s) * (2.0 * GELU_A + (6.0 * GELU_B) * sq)
        act_ref[:, sl] = act.astype(BF)
        d_pre = (ga_ref[:, sl] * slope).astype(BF)
        dpre_ref[:, sl] = d_pre
        term = dot(d_pre, wit_ref[sl, :])
        total = term if total is None else total + term
    d_hidden = total.astype(BF)
    for b in range(block):
        lines = pl.ds(i * block + b, modes, stride=half)
        sums = dot(invt_ref[...], d_hidden[b * cols : (b + 1) * cols])
        part_lo[lines, :] = sums[:, :LANES]
        part_hi[lines, :] = sums[:, LANES:]

    @pl.when(i == pl.num_programs(0) - 1)
    def _():
        part_ref[:, :LANES] = part_lo[...].astype(BF)
        part_ref[:, LANES:] = part_hi[...].astype(BF)


def mlp_call(mix, ga, inv, w_in, block=2):
    cols, modes = inv.shape
    chan, width = w_in.shape
    half = mix.shape[0] // modes
    rows = block * cols
    whole = lambda i: (0, 0)
    step = lambda i: (i, 0)
    return pl.pallas_call(
        mlp_kernel,
        grid=(half // block,),
        in_specs=[
            pl.BlockSpec((modes * half, chan), whole),
            pl.BlockSpec((rows, width), step),
            pl.BlockSpec((cols, modes), whole),
            pl.BlockSpec((modes, cols), whole),
            pl.BlockSpec((chan, width), whole),
            pl.BlockSpec((width, chan), whole),
        ],
        out_specs=[
            pl.BlockSpec((rows, chan), step),
            pl.BlockSpec((rows, width), step),
            pl.BlockSpec((rows, width), step),
            pl.BlockSpec((modes * half, chan), whole),
        ],
        out_shape=[
            jax.ShapeDtypeStruct((half * cols, chan), BF),
            jax.ShapeDtypeStruct((half * cols, width), BF),
            jax.ShapeDtypeStruct((half * cols, width), BF),
            jax.ShapeDtypeStruct((modes * half, chan), BF),
        ],
        scratch_shapes=[pltpu.VMEM((modes * half, LANES), F32)] * 4,
        name="mlp",
    )(mix, ga, inv, inv.T, w_in, w_in.T)


def grads_kernel(core_ref, hid_ref, dpre_ref, act_ref, own_ref, par_ref, keep_ref, send_ref, acc_in, acc_out):
    i = pl.program_id(0)
    block, _, _ = own_ref.shape
    chips, kept, _ = keep_ref.shape
    groups = kept // 8

    @pl.when(i == 0)
    def _():
        acc_in[...] = jnp.zeros_like(acc_in)
        acc_out[...] = jnp.zeros_like(acc_out)

    acc_in[...] += rows_dot(hid_ref[...], dpre_ref[...])
    cot = jnp.concatenate([r[b] for b in range(block) for r in (own_ref, par_ref)], axis=0)
    acc_out[...] += rows_dot(cot, act_ref[...])

    def store(ref, acc):
        full = acc[...].T
        for t in range(chips):
            for g in range(groups):
                top = (g * chips + t) * 8
                if ref.dtype == F32:
                    ref[t, g * 8 : (g + 1) * 8, :] = full[top : top + 8]
            if ref.dtype != F32:
                ref[t] = jnp.concatenate(
                    [full[(g * chips + t) * 8 : (g * chips + t) * 8 + 8] for g in range(groups)], axis=0
                ).astype(ref.dtype)

    last = i == pl.num_programs(0) - 1

    @pl.when(last & (core_ref[0] == 0))
    def _():
        store(keep_ref, acc_in)
        store(send_ref, acc_out)

    @pl.when(last & (core_ref[0] != 0))
    def _():
        store(keep_ref, acc_out)
        store(send_ref, acc_in)


def grads_call(core, hidden, d_pre, act, own, par, chips, block=4):
    half, cols, chan = own.shape
    width = act.shape[1]
    rows = block * 2 * cols
    kept = width // chips
    step = lambda i, c: (i, 0)
    line = lambda i, c: (i, 0, 0)
    whole = lambda i, c: (0, 0, 0)
    return pl.pallas_call(
        grads_kernel,
        grid_spec=pltpu.PrefetchScalarGridSpec(
            num_scalar_prefetch=1,
            grid=(half // block,),
            in_specs=[
                pl.BlockSpec((rows, chan), step),
                pl.BlockSpec((rows, width), step),
                pl.BlockSpec((rows, width), step),
                pl.BlockSpec((block, cols, chan), line),
                pl.BlockSpec((block, cols, chan), line),
            ],
            out_specs=[
                pl.BlockSpec((chips, kept, chan), whole),
                pl.BlockSpec((chips, kept, chan), whole),
            ],
            scratch_shapes=[pltpu.VMEM((chan, width), F32), pltpu.VMEM((chan, width), F32)],
        ),
        out_shape=[
            jax.ShapeDtypeStruct((chips, kept, chan), F32),
            jax.ShapeDtypeStruct((chips, kept, chan), BF),
        ],
        name="grads",
    )(core.reshape(1), hidden, d_pre, act, own, par)


def local(inputs, cotangent, mode_weight, w_in, w_out):
    lines, cols, chan = inputs.shape
    nx = lax.axis_size("gx")
    ny = lax.axis_size("gy")
    chips = nx // 2
    total_x = cols * nx
    half = lines // 2
    own_rows = chan // nx
    me = lax.axis_index("gx")
    core = me % 2
    groups = [[2 * t + c for t in range(chips)] for c in range(2)]
    swap = [(i, i ^ 1) for i in range(nx)]

    def pair(x):
        return lax.ppermute(x, "gx", swap)

    def spread(x):
        return lax.all_to_all(x, "gx", 0, 0, tiled=True, axis_index_groups=groups)

    def pick(x, which, axis):
        return lax.dynamic_index_in_dim(x, which, axis, keepdims=False)

    inp2 = inputs.reshape(2, half, cols, chan)
    cot2 = cotangent.reshape(2, half, cols, chan)
    in_par = pair(pick(inp2, 1 - core, 0))
    cot_par = pair(pick(cot2, 1 - core, 0))
    in_own = pick(inp2, core, 0)
    cot_own = pick(cot2, core, 0)
    steps = jnp.arange(cols, dtype=jnp.int32)
    own_fwd, own_inv = bases(me * cols + steps, total_x, M)
    par_fwd, par_inv = bases((me ^ 1) * cols + steps, total_x, M)
    inv = jnp.concatenate([own_inv, par_inv], axis=0)

    spec_part = contract("yxc,xm->myc", in_own, own_fwd) + contract("yxc,xm->myc", in_par, par_fwd)
    spec_part = spec_part.astype(BF).reshape(chips, 2 * half, chan)
    weight_rows = mode_weight.transpose(1, 0, 2, 3).reshape(M, 2 * own_rows, chan)
    recv = spread(jnp.concatenate([spec_part, weight_rows], axis=1))
    grad_act = grad_act_call(cot_own, cot_par, w_out.T)
    spec = recv[:, : 2 * half].astype(F32).sum(0).astype(BF).reshape(2, half, chan)
    w_mine = recv[:, 2 * half :].reshape(chips, 2, own_rows, chan)
    w_par = pair(w_mine)
    w_even = jnp.where(core == 0, w_mine, w_par)
    w_odd = jnp.where(core == 0, w_par, w_mine)
    w_all = jnp.stack([w_even, w_odd], axis=1).transpose(2, 0, 1, 3, 4).reshape(2, chan, chan)
    w_re, w_im = w_all[0], w_all[1]
    u_re, u_im = spec[0], spec[1]
    vr = contract("yc,co->yo", u_re, w_re) - contract("yc,co->yo", u_im, w_im)
    vi = contract("yc,co->yo", u_re, w_im) + contract("yc,co->yo", u_im, w_re)
    mixed = jnp.concatenate([vr, vi], axis=0).astype(BF)
    mixed = spread(jnp.broadcast_to(mixed[None], (chips, 2 * half, chan)))
    spec_par = pair(spec)

    hidden, act, d_pre, d_part = mlp_call(mixed.reshape(2 * M * half, chan), grad_act, inv, w_in)
    dv = spread(d_part.reshape(chips, 2 * half, chan))
    g_own, g_send = grads_call(core, hidden, d_pre, act, cot_own, cot_par, chips)
    g_par = pair(g_send)
    dv = dv.astype(F32).sum(0).astype(BF).reshape(2, half, chan)
    dv_par = pair(dv)
    d_re, d_im = dv[0], dv[1]
    du_re = contract("yo,co->yc", d_re, w_re) + contract("yo,co->yc", d_im, w_im)
    du_im = contract("yo,co->yc", d_im, w_re) - contract("yo,co->yc", d_re, w_im)
    du = jnp.concatenate([du_re, du_im], axis=0).astype(BF)
    u_all = jnp.concatenate([spec, spec_par], axis=1)
    d_all = jnp.concatenate([dv, dv_par], axis=1)
    g_re = contract("yc,yo->co", u_all[0], d_all[0]) + contract("yc,yo->co", u_all[1], d_all[1])
    g_im = contract("yc,yo->co", u_all[0], d_all[1]) - contract("yc,yo->co", u_all[1], d_all[0])
    mode_rows = jnp.stack([g_re, g_im], axis=0).astype(BF).reshape(2, chips, 2, own_rows, chan)
    mode_rows = pick(mode_rows, core, 2).transpose(1, 0, 2, 3).reshape(chips, 2 * own_rows, chan)
    g_rows = (g_own + g_par.astype(F32)).astype(BF)
    du_rows = jnp.broadcast_to(du[None], (chips, 2 * half, chan))
    recv = spread(jnp.concatenate([du_rows, g_rows, mode_rows], axis=1))
    du_own = recv[:, : 2 * half]
    recv = recv[:, 2 * half :]
    du_par = pair(du_own)
    cut = g_rows.shape[1]
    g_all = recv[:, :cut].astype(F32).sum(0).astype(BF).reshape(ny, 2 * own_rows, chan)
    mode_part = recv[:, cut:].reshape(ny, (M // ny) * 2 * own_rows, chan)
    blocks = jnp.concatenate([g_all, mode_part], axis=1)
    total = lax.all_to_all(blocks, "gy", 0, 0, tiled=True)
    total = total.astype(F32).sum(0)
    mine, other = total[: 2 * own_rows], total[2 * own_rows :]
    mine = mine.reshape(2, own_rows, chan)
    swapped = pair(pick(mine, 1 - core, 0))
    mine = pick(mine, core, 0)
    tail_in = jnp.where(core == 0, mine, swapped)
    tail_out = jnp.where(core == 0, swapped, mine)
    d_mode = other.reshape(M // ny, 2, own_rows, chan).transpose(1, 0, 2, 3)

    du_lo = jnp.where(core == 0, du_own, du_par).reshape(2 * M, half, chan)
    du_hi = jnp.where(core == 0, du_par, du_own).reshape(2 * M, half, chan)
    ret_lo = contract("myc,xm->yxc", du_lo, own_fwd)
    ret_hi = contract("myc,xm->yxc", du_hi, own_fwd)
    returned = jnp.concatenate([ret_lo, ret_hi], axis=0)
    d_inputs = (cotangent.astype(F32) + returned).astype(BF)
    scale_mlp = 1.0 / math.sqrt(lines * ny * total_x)
    scale_mode = 1.0 / math.sqrt(lines * ny)
    return (d_inputs, d_mode * scale_mode, tail_in.T * scale_mlp, tail_out * scale_mlp)


def solution(mesh):
    placed = (P("gy", "gx", None), P("gy", "gx", None), P(None, None, "gx", None), P(), P())
    return jax.shard_map(
        local,
        mesh=mesh,
        in_specs=placed,
        out_specs=(
            P("gy", "gx", None),
            P(None, "gy", "gx", None),
            P(None, ("gy", "gx")),
            P(("gy", "gx"), None),
        ),
        check_vma=False,
    )
```

```python
import math

import jax
import jax.numpy as jnp
from jax import lax
from jax.experimental import pallas as pl
from jax.experimental.pallas import tpu as pltpu
from jax.sharding import PartitionSpec as P

M = 32
LANES = 128
BF = jnp.bfloat16
F32 = jnp.float32


def bases(positions, length, modes):
    order = jnp.arange(modes, dtype=jnp.int32)
    phase = positions[:, None] * order[None, :] % length
    angle = phase.astype(F32) * (2.0 * math.pi / length)
    factor = 1.0 / math.sqrt(length)
    cosine = jnp.cos(angle) * factor
    sine = jnp.sin(angle) * factor
    weight = jnp.where(order == 0, 1.0, 2.0).astype(F32)
    forward = jnp.stack([cosine, -sine], axis=2).astype(BF)
    inverse = jnp.stack([cosine * weight, -sine * weight], axis=2).astype(BF)
    size = positions.shape[0]
    return forward.reshape(size, 2 * modes), inverse.reshape(size, 2 * modes)


def contract(form, left, right):
    return jnp.einsum(form, left, right, preferred_element_type=F32)


def dot(left, right):
    return jnp.dot(left, right, preferred_element_type=F32)


def rows_dot(left, right):
    return lax.dot_general(left, right, (((0,), (0,)), ((), ())), preferred_element_type=F32)


GELU_A = math.sqrt(2.0 / math.pi)
GELU_B = 0.044715 * GELU_A


def mlp_kernel(
    mix_ref, own_ref, par_ref, inv_ref, invt_ref, wi_ref, wit_ref, wot_ref,
    hid_ref, act_ref, dpre_ref, part_ref,
    mix_lo, mix_hi, part_lo, part_hi, pre_s, ga_s, dh_s,
):
    i = pl.program_id(0)
    block, cols, chan = own_ref.shape
    modes = inv_ref.shape[1]
    half = mix_ref.shape[0] // modes
    side = block * cols
    chunk = 32

    @pl.when(i == 0)
    def _():
        mix_lo[...] = mix_ref[:, :LANES].astype(F32)
        mix_hi[...] = mix_ref[:, LANES:].astype(F32)

    for b in range(block):
        lines = pl.ds(i * block + b, modes, stride=half)
        table = jnp.concatenate([mix_lo[lines, :], mix_hi[lines, :]], axis=1).astype(BF)
        h = dot(inv_ref[...], table).astype(BF)
        hid_ref[b * cols : (b + 1) * cols, :] = h[:cols]
        hid_ref[side + b * cols : side + (b + 1) * cols, :] = h[cols:]
    for k, ref in ((0, own_ref), (1, par_ref)):
        rows = slice(k * side, (k + 1) * side)
        pre_s[k] = dot(hid_ref[rows, :], wi_ref[...])
        ga_s[k] = dot(ref[...].reshape(side, chan), wot_ref[...])
        for r in range(0, side, chunk):
            p = pre_s[k, r : r + chunk, :]
            g = ga_s[k, r : r + chunk, :]
            sq = p * p
            t = 0.5 * jnp.tanh(p * (GELU_A + GELU_B * sq))
            s = 0.5 + t
            a = p * s
            slope = s + (a * (0.5 - t)) * (2.0 * GELU_A + (6.0 * GELU_B) * sq)
            there = slice(k * side + r, k * side + r + chunk)
            act_ref[there, :] = a.astype(BF)
            dpre_ref[there, :] = (g * slope).astype(BF)
        dh_s[rows, :] = dot(dpre_ref[rows, :], wit_ref[...])
    for b in range(block):
        lines = pl.ds(i * block + b, modes, stride=half)
        mine = dh_s[b * cols : (b + 1) * cols, :]
        other = dh_s[side + b * cols : side + (b + 1) * cols, :]
        sums = dot(invt_ref[...], jnp.concatenate([mine, other], axis=0).astype(BF))
        part_lo[lines, :] = sums[:, :LANES]
        part_hi[lines, :] = sums[:, LANES:]

    @pl.when(i == pl.num_programs(0) - 1)
    def _():
        part_ref[:, :LANES] = part_lo[...].astype(BF)
        part_ref[:, LANES:] = part_hi[...].astype(BF)


def mlp_call(mix, own, par, inv, w_in, w_out_t, block=4):
    half, cols, chan = own.shape
    modes = inv.shape[1]
    width = w_in.shape[1]
    rows = 2 * block * cols
    whole = lambda i: (0, 0)
    step = lambda i: (i, 0)
    line = lambda i: (i, 0, 0)
    return pl.pallas_call(
        mlp_kernel,
        grid=(half // block,),
        in_specs=[
            pl.BlockSpec((modes * half, chan), whole),
            pl.BlockSpec((block, cols, chan), line),
            pl.BlockSpec((block, cols, chan), line),
            pl.BlockSpec((2 * cols, modes), whole),
            pl.BlockSpec((modes, 2 * cols), whole),
            pl.BlockSpec((chan, width), whole),
            pl.BlockSpec((width, chan), whole),
            pl.BlockSpec((chan, width), whole),
        ],
        out_specs=[
            pl.BlockSpec((rows, chan), step),
            pl.BlockSpec((rows, width), step),
            pl.BlockSpec((rows, width), step),
            pl.BlockSpec((modes * half, chan), whole),
        ],
        out_shape=[
            pltpu.HBM((2 * half * cols, chan), BF),
            pltpu.HBM((2 * half * cols, width), BF),
            pltpu.HBM((2 * half * cols, width), BF),
            pltpu.HBM((modes * half, chan), BF),
        ],
        scratch_shapes=[pltpu.VMEM((modes * half, LANES), F32)] * 4
        + [pltpu.VMEM((2, block * cols, width), F32)] * 2
        + [pltpu.VMEM((rows, chan), F32)],
        compiler_params=pltpu.CompilerParams(vmem_limit_bytes=30 << 20),
        name="mlp",
    )(mix, own, par, inv, inv.T, w_in, w_in.T, w_out_t)


def grads_kernel(core_ref, hid_ref, dpre_ref, act_ref, own_ref, par_ref, keep_ref, send_ref, acc_in, acc_out):
    i = pl.program_id(0)
    block, cols, _ = own_ref.shape
    chips, kept, _ = keep_ref.shape
    groups = kept // 8

    @pl.when(i == 0)
    def _():
        acc_in[...] = jnp.zeros_like(acc_in)
        acc_out[...] = jnp.zeros_like(acc_out)

    acc_in[...] += rows_dot(hid_ref[...], dpre_ref[...])
    flat = (block * cols, own_ref.shape[2])
    cot = jnp.concatenate([own_ref[...].reshape(flat), par_ref[...].reshape(flat)], axis=0)
    acc_out[...] += rows_dot(cot, act_ref[...])

    def store(ref, acc):
        full = acc[...].T
        for t in range(chips):
            for g in range(groups):
                top = (g * chips + t) * 8
                if ref.dtype == F32:
                    ref[t, g * 8 : (g + 1) * 8, :] = full[top : top + 8]
            if ref.dtype != F32:
                ref[t] = jnp.concatenate(
                    [full[(g * chips + t) * 8 : (g * chips + t) * 8 + 8] for g in range(groups)], axis=0
                ).astype(ref.dtype)

    last = i == pl.num_programs(0) - 1

    @pl.when(last & (core_ref[0] == 0))
    def _():
        store(keep_ref, acc_in)
        store(send_ref, acc_out)

    @pl.when(last & (core_ref[0] != 0))
    def _():
        store(keep_ref, acc_out)
        store(send_ref, acc_in)


def in_hbm(x):
    return pltpu.with_memory_space_constraint(x, pltpu.HBM)


def grads_call(core, hidden, d_pre, act, own, par, chips, block=4):
    half, cols, chan = own.shape
    width = act.shape[1]
    rows = block * 2 * cols
    kept = width // chips
    step = lambda i, c: (i, 0)
    line = lambda i, c: (i, 0, 0)
    whole = lambda i, c: (0, 0, 0)
    return pl.pallas_call(
        grads_kernel,
        grid_spec=pltpu.PrefetchScalarGridSpec(
            num_scalar_prefetch=1,
            grid=(half // block,),
            in_specs=[
                pl.BlockSpec((rows, chan), step),
                pl.BlockSpec((rows, width), step),
                pl.BlockSpec((rows, width), step),
                pl.BlockSpec((block, cols, chan), line),
                pl.BlockSpec((block, cols, chan), line),
            ],
            out_specs=[
                pl.BlockSpec((chips, kept, chan), whole),
                pl.BlockSpec((chips, kept, chan), whole),
            ],
            scratch_shapes=[pltpu.VMEM((chan, width), F32), pltpu.VMEM((chan, width), F32)],
        ),
        out_shape=[
            jax.ShapeDtypeStruct((chips, kept, chan), F32),
            jax.ShapeDtypeStruct((chips, kept, chan), BF),
        ],
        compiler_params=pltpu.CompilerParams(vmem_limit_bytes=26 << 20),
        name="grads",
    )(core.reshape(1), in_hbm(hidden), in_hbm(d_pre), in_hbm(act), own, par)


def sum_kernel(recv_ref, out_ref):
    total = recv_ref[0].astype(F32)
    for t in range(1, recv_ref.shape[0]):
        total = total + recv_ref[t].astype(F32)
    out_ref[...] = total.astype(BF)


def sum_call(recv, rows):
    chips, _, chan = recv.shape
    return pl.pallas_call(
        sum_kernel,
        grid=(1,),
        in_specs=[pl.BlockSpec((chips, rows, chan), lambda i: (0, 0, 0))],
        out_specs=pl.BlockSpec((rows, chan), lambda i: (0, 0)),
        out_shape=jax.ShapeDtypeStruct((rows, chan), BF),
        compiler_params=pltpu.CompilerParams(vmem_limit_bytes=6 << 20),
        name="sum_parts",
    )(recv)


def by_half(low, high):
    row = lax.broadcasted_iota(jnp.int32, low.shape, 1)
    return jnp.where(row < 4, low, high)


def mix_kernel(core_ref, u_ref, own_ref, par_ref, out_ref, re_ref, im_ref):
    even = core_ref[0] == 0
    own = own_ref[...].astype(F32)
    par = par_ref[...].astype(F32)
    first = jnp.where(even, own, par)
    second = jnp.where(even, par, own)
    chan = re_ref.shape[0]
    re_ref[...] = by_half(first, pltpu.roll(second, 4, 1)).reshape(chan, chan).astype(BF)
    im_ref[...] = by_half(pltpu.roll(first, 4, 1), second).reshape(chan, chan).astype(BF)
    half = u_ref.shape[0] // 2
    by_re = dot(u_ref[...], re_ref[...])
    by_im = dot(u_ref[...], im_ref[...])
    vr = by_re[:half] - by_im[half:]
    vi = by_re[half:] + by_im[:half]
    mixed = jnp.concatenate([vr, vi], axis=0).astype(BF)
    for t in range(out_ref.shape[0]):
        out_ref[t] = mixed


def mix_call(core, u, own, par):
    chips, _, chan = own.shape
    vmem = pl.BlockSpec(memory_space=pltpu.VMEM)
    return pl.pallas_call(
        mix_kernel,
        in_specs=[pl.BlockSpec(memory_space=pltpu.SMEM), vmem, vmem, vmem],
        out_specs=[vmem, vmem, vmem],
        out_shape=[
            pltpu.HBM((chips, u.shape[0], chan), BF),
            pltpu.HBM((chan, chan), BF),
            pltpu.HBM((chan, chan), BF),
        ],
        compiler_params=pltpu.CompilerParams(vmem_limit_bytes=8 << 20),
        name="mix",
    )(core.reshape(1), u, own, par)


def last_kernel(core_ref, u_ref, upar_ref, d_ref, dpar_ref, re_ref, im_ref, gown_ref, gpar_ref, out_ref, du_ref):
    even = core_ref[0] == 0
    both = d_ref.shape[0]
    half = both // 2
    chips, kept, chan = gown_ref.shape
    across = (((1,), (1,)), ((), ()))
    by_re = lax.dot_general(d_ref[...], re_ref[...], across, preferred_element_type=F32)
    by_im = lax.dot_general(d_ref[...], im_ref[...], across, preferred_element_type=F32)
    du_re = by_re[:half] + by_im[half:]
    du_im = by_re[half:] - by_im[:half]
    du = jnp.concatenate([du_re, du_im], axis=0).astype(BF)
    u_re = jnp.concatenate([u_ref[:half], upar_ref[:half]], axis=0)
    u_im = jnp.concatenate([u_ref[half:], upar_ref[half:]], axis=0)
    d_re = jnp.concatenate([d_ref[:half], dpar_ref[:half]], axis=0)
    d_im = jnp.concatenate([d_ref[half:], dpar_ref[half:]], axis=0)
    u_all = jnp.concatenate([u_re, u_im], axis=0)
    g_re = rows_dot(u_all, jnp.concatenate([d_re, d_im], axis=0)).reshape(chips, 8, chan)
    g_im = rows_dot(u_all, jnp.concatenate([d_im, -d_re], axis=0)).reshape(chips, 8, chan)
    low = jnp.where(even, g_re, pltpu.roll(g_re, 4, 1))
    high = jnp.where(even, pltpu.roll(g_im, 4, 1), g_im)
    out_ref[:, kept:, :] = by_half(low, high).astype(BF)
    for t in range(chips):
        du_ref[t] = du
        out_ref[t, :kept, :] = (gown_ref[t] + gpar_ref[t].astype(F32)).astype(BF)


def last_call(core, u, u_par, d, d_par, w_re, w_im, g_own, g_par):
    chips, kept, chan = g_own.shape
    vmem = pl.BlockSpec(memory_space=pltpu.VMEM)
    return pl.pallas_call(
        last_kernel,
        in_specs=[pl.BlockSpec(memory_space=pltpu.SMEM)] + [vmem] * 8,
        out_specs=[vmem, vmem],
        out_shape=[
            jax.ShapeDtypeStruct((chips, kept + 8, chan), BF),
            jax.ShapeDtypeStruct((chips, d.shape[0], chan), BF),
        ],
        compiler_params=pltpu.CompilerParams(vmem_limit_bytes=14 << 20),
        name="last",
    )(core.reshape(1), u, u_par, d, d_par, w_re, w_im, g_own, g_par)


def lines_kernel(recv_ref, out_ref):
    groups, _, _ = out_ref.shape
    chips, kept, _ = recv_ref.shape
    own = kept - 8
    total = recv_ref[0, :own, :].astype(F32)
    for t in range(1, chips):
        total = total + recv_ref[t, :own, :].astype(F32)
    per = chips // groups
    for g in range(groups):
        parts = [total[8 * g : 8 * g + 8]]
        parts += [recv_ref[t, own:, :].astype(F32) for t in range(g * per, (g + 1) * per)]
        out_ref[g] = jnp.concatenate(parts, axis=0).astype(BF)


def lines_call(recv, groups):
    chips, _, chan = recv.shape
    per = chips // groups
    vmem = pl.BlockSpec(memory_space=pltpu.VMEM)
    return pl.pallas_call(
        lines_kernel,
        in_specs=[vmem],
        out_specs=vmem,
        out_shape=jax.ShapeDtypeStruct((groups, 8 + 8 * per, chan), BF),
        compiler_params=pltpu.CompilerParams(vmem_limit_bytes=8 << 20),
        name="lines_rows",
    )(recv)


def local(inputs, cotangent, mode_weight, w_in, w_out):
    lines, cols, chan = inputs.shape
    nx = lax.axis_size("gx")
    ny = lax.axis_size("gy")
    chips = nx // 2
    total_x = cols * nx
    half = lines // 2
    own_rows = chan // nx
    me = lax.axis_index("gx")
    gy = lax.axis_index("gy")
    core = me % 2
    groups = [[2 * t + c for t in range(chips)] for c in range(2)]
    swap = [(i, i ^ 1) for i in range(nx)]

    def pair(x):
        return lax.ppermute(x, "gx", swap)

    def spread(x):
        return lax.all_to_all(x, "gx", 0, 0, tiled=True, axis_index_groups=groups)

    def pick(x, which, axis):
        return lax.dynamic_index_in_dim(x, which, axis, keepdims=False)

    inp2 = inputs.reshape(2, half, cols, chan)
    cot2 = cotangent.reshape(2, half, cols, chan)
    in_par = pair(pick(inp2, 1 - core, 0))
    cot_par = pair(pick(cot2, 1 - core, 0))
    in_own = pick(inp2, core, 0)
    cot_own = pick(cot2, core, 0)
    steps = jnp.arange(cols, dtype=jnp.int32)
    own_fwd, own_inv = bases(me * cols + steps, total_x, M)
    par_fwd, par_inv = bases((me ^ 1) * cols + steps, total_x, M)
    inv = jnp.concatenate([own_inv, par_inv], axis=0)

    spec_part = contract("yxc,xm->myc", in_own, own_fwd) + contract("yxc,xm->myc", in_par, par_fwd)
    spec_part = spec_part.astype(BF).reshape(chips, 2 * half, chan)
    weight_rows = mode_weight.transpose(1, 0, 2, 3).reshape(M, 2 * own_rows, chan)
    recv = spread(jnp.concatenate([spec_part, weight_rows], axis=1))
    both = 2 * half
    w_mine = recv[:, both:]
    w_par = pair(w_mine)
    spec = sum_call(recv, both)
    sent, w_re, w_im = mix_call(core, spec, w_mine, w_par)
    mixed = spread(sent)
    spec_par = pair(spec)
    hidden, act, d_pre, d_part = mlp_call(
        mixed.reshape(2 * M * half, chan), cot_own, cot_par, inv, w_in, w_out.T
    )
    dv = spread(d_part.reshape(chips, both, chan))
    g_own, g_send = grads_call(core, hidden, d_pre, act, cot_own, cot_par, chips)
    g_par = pair(g_send)
    dv = sum_call(dv, both)
    dv_par = pair(dv)
    sent, du = last_call(core, spec, spec_par, dv, dv_par, w_re, w_im, g_own, g_par)
    recv = spread(sent)
    recv, du = lax.optimization_barrier((recv, du))
    du_own = spread(du)
    du_par = pair(du_own)
    blocks = lines_call(recv, ny)
    total = pick(blocks, gy, 0).astype(F32)
    for d in range(1, ny):
        sent = pick(blocks, (gy + d) % ny, 0)
        moved = lax.ppermute(sent, "gy", [(i, (i + d) % ny) for i in range(ny)])
        total = total + moved.astype(F32)
    mine, other = total[: 2 * own_rows], total[2 * own_rows :]
    mine = mine.reshape(2, own_rows, chan)
    swapped = pair(pick(mine, 1 - core, 0))
    mine = pick(mine, core, 0)
    tail_in = jnp.where(core == 0, mine, swapped)
    tail_out = jnp.where(core == 0, swapped, mine)
    d_mode = other.reshape(M // ny, 2, own_rows, chan).transpose(1, 0, 2, 3)

    du_lo = jnp.where(core == 0, du_own, du_par).reshape(2 * M, half, chan)
    du_hi = jnp.where(core == 0, du_par, du_own).reshape(2 * M, half, chan)
    ret_lo = contract("myc,xm->yxc", du_lo, own_fwd)
    ret_hi = contract("myc,xm->yxc", du_hi, own_fwd)
    returned = jnp.concatenate([ret_lo, ret_hi], axis=0)
    d_inputs = (cotangent.astype(F32) + returned).astype(BF)
    scale_mlp = 1.0 / math.sqrt(lines * ny * total_x)
    scale_mode = 1.0 / math.sqrt(lines * ny)
    return (d_inputs, d_mode * scale_mode, tail_in.T * scale_mlp, tail_out * scale_mlp)


def solution(mesh):
    placed = (P("gy", "gx", None), P("gy", "gx", None), P(None, None, "gx", None), P(), P())
    return jax.shard_map(
        local,
        mesh=mesh,
        in_specs=placed,
        out_specs=(
            P("gy", "gx", None),
            P(None, "gy", "gx", None),
            P(None, ("gy", "gx")),
            P(("gy", "gx"), None),
        ),
        check_vma=False,
    )
```

```python
import functools
import math

import jax
import jax.numpy as jnp
from jax import lax
from jax.experimental import pallas as pl
from jax.experimental.pallas import tpu as pltpu
from jax.sharding import PartitionSpec as P

M = 32
LANES = 128
BF = jnp.bfloat16
F32 = jnp.float32


def bases(positions, length, modes):
    order = jnp.arange(modes, dtype=jnp.int32)
    phase = positions[:, None] * order[None, :] % length
    angle = phase.astype(F32) * (2.0 * math.pi / length)
    factor = 1.0 / math.sqrt(length)
    cosine = jnp.cos(angle) * factor
    sine = jnp.sin(angle) * factor
    weight = jnp.where(order == 0, 1.0, 2.0).astype(F32)
    forward = jnp.stack([cosine, -sine], axis=2).astype(BF)
    inverse = jnp.stack([cosine * weight, -sine * weight], axis=2).astype(BF)
    size = positions.shape[0]
    return forward.reshape(size, 2 * modes), inverse.reshape(size, 2 * modes)


def contract(form, left, right):
    return jnp.einsum(form, left, right, preferred_element_type=F32)


def dot(left, right):
    return jnp.dot(left, right, preferred_element_type=F32)


def rows_dot(left, right):
    return lax.dot_general(left, right, (((0,), (0,)), ((), ())), preferred_element_type=F32)


GELU_A = math.sqrt(2.0 / math.pi)
GELU_B = 0.044715 * GELU_A


def mlp_kernel(
    mix_ref, own_ref, par_ref, inv_ref, invt_ref, wi_ref, wit_ref, wot_ref,
    hid_ref, act_ref, dpre_ref, part_ref,
    mix_lo, mix_hi, part_lo, part_hi, pre_s, ga_s, dh_s,
):
    i = pl.program_id(0)
    block, cols, chan = own_ref.shape
    modes = inv_ref.shape[1]
    half = mix_ref.shape[0] // modes
    side = block * cols
    chunk = 32

    @pl.when(i == 0)
    def _():
        mix_lo[...] = mix_ref[:, :LANES].astype(F32)
        mix_hi[...] = mix_ref[:, LANES:].astype(F32)

    for b in range(block):
        lines = pl.ds(i * block + b, modes, stride=half)
        table = jnp.concatenate([mix_lo[lines, :], mix_hi[lines, :]], axis=1).astype(BF)
        h = dot(inv_ref[...], table).astype(BF)
        hid_ref[b * cols : (b + 1) * cols, :] = h[:cols]
        hid_ref[side + b * cols : side + (b + 1) * cols, :] = h[cols:]
    for k, ref in ((0, own_ref), (1, par_ref)):
        rows = slice(k * side, (k + 1) * side)
        pre_s[k] = dot(hid_ref[rows, :], wi_ref[...])
        ga_s[k] = dot(ref[...].reshape(side, chan), wot_ref[...])
        for r in range(0, side, chunk):
            p = pre_s[k, r : r + chunk, :]
            g = ga_s[k, r : r + chunk, :]
            sq = p * p
            t = 0.5 * jnp.tanh(p * (GELU_A + GELU_B * sq))
            s = 0.5 + t
            a = p * s
            slope = s + (a * (0.5 - t)) * (2.0 * GELU_A + (6.0 * GELU_B) * sq)
            there = slice(k * side + r, k * side + r + chunk)
            act_ref[there, :] = a.astype(BF)
            dpre_ref[there, :] = (g * slope).astype(BF)
        dh_s[rows, :] = dot(dpre_ref[rows, :], wit_ref[...])
    for b in range(block):
        lines = pl.ds(i * block + b, modes, stride=half)
        mine = dh_s[b * cols : (b + 1) * cols, :]
        other = dh_s[side + b * cols : side + (b + 1) * cols, :]
        sums = dot(invt_ref[...], jnp.concatenate([mine, other], axis=0).astype(BF))
        part_lo[lines, :] = sums[:, :LANES]
        part_hi[lines, :] = sums[:, LANES:]

    @pl.when(i == pl.num_programs(0) - 1)
    def _():
        part_ref[:, :LANES] = part_lo[...].astype(BF)
        part_ref[:, LANES:] = part_hi[...].astype(BF)


def mlp_call(mix, own, par, inv, w_in, w_out_t, block=4):
    half, cols, chan = own.shape
    modes = inv.shape[1]
    width = w_in.shape[1]
    rows = 2 * block * cols
    whole = lambda i: (0, 0)
    step = lambda i: (i, 0)
    line = lambda i: (i, 0, 0)
    return pl.pallas_call(
        mlp_kernel,
        grid=(half // block,),
        in_specs=[
            pl.BlockSpec((modes * half, chan), whole),
            pl.BlockSpec((block, cols, chan), line),
            pl.BlockSpec((block, cols, chan), line),
            pl.BlockSpec((2 * cols, modes), whole),
            pl.BlockSpec((modes, 2 * cols), whole),
            pl.BlockSpec((chan, width), whole),
            pl.BlockSpec((width, chan), whole),
            pl.BlockSpec((chan, width), whole),
        ],
        out_specs=[
            pl.BlockSpec((rows, chan), step),
            pl.BlockSpec((rows, width), step),
            pl.BlockSpec((rows, width), step),
            pl.BlockSpec((modes * half, chan), whole),
        ],
        out_shape=[
            pltpu.HBM((2 * half * cols, chan), BF),
            pltpu.HBM((2 * half * cols, width), BF),
            pltpu.HBM((2 * half * cols, width), BF),
            pltpu.HBM((modes * half, chan), BF),
        ],
        scratch_shapes=[pltpu.VMEM((modes * half, LANES), F32)] * 4
        + [pltpu.VMEM((2, block * cols, width), F32)] * 2
        + [pltpu.VMEM((rows, chan), F32)],
        compiler_params=pltpu.CompilerParams(vmem_limit_bytes=30 << 20),
        name="mlp",
    )(mix, own, par, inv, inv.T, w_in, w_in.T, w_out_t)


def by_half(low, high):
    row = lax.broadcasted_iota(jnp.int32, low.shape, 1)
    return jnp.where(row < 4, low, high)


def grads_kernel(core_ref, hid_ref, dpre_ref, act_ref, own_ref, par_ref, keep_ref, send_ref, acc_in, acc_out):
    i = pl.program_id(0)
    block, cols, chan = own_ref.shape
    chips, kept, chan = keep_ref.shape
    groups = kept // 8

    @pl.when(i == 0)
    def _():
        acc_in[...] = jnp.zeros_like(acc_in)
        acc_out[...] = jnp.zeros_like(acc_out)

    acc_in[...] += rows_dot(hid_ref[...], dpre_ref[...])
    flat = (block * cols, own_ref.shape[2])
    cot = jnp.concatenate([own_ref[...].reshape(flat), par_ref[...].reshape(flat)], axis=0)
    acc_out[...] += rows_dot(cot, act_ref[...])

    @pl.when(i == pl.num_programs(0) - 1)
    def _():
        even = core_ref[0] == 0
        g_in = acc_in[...].T.reshape(groups * chips, 8, chan)
        g_out = acc_out[...].T.reshape(groups * chips, 8, chan)
        lows = by_half(g_in, pltpu.roll(g_out, 4, 1))
        highs = by_half(pltpu.roll(g_in, 4, 1), g_out)
        keep = jnp.where(even, lows, highs)
        send = jnp.where(even, highs, lows)
        for t in range(chips):
            keep_ref[t] = jnp.concatenate([keep[g * chips + t] for g in range(groups)], axis=0)
            send_ref[t] = jnp.concatenate([send[g * chips + t] for g in range(groups)], axis=0).astype(BF)


def in_hbm(x):
    return pltpu.with_memory_space_constraint(x, pltpu.HBM)


def grads_call(core, hidden, d_pre, act, own, par, chips, block=4):
    half, cols, chan = own.shape
    width = act.shape[1]
    rows = block * 2 * cols
    kept = width // chips
    step = lambda i, c: (i, 0)
    line = lambda i, c: (i, 0, 0)
    whole = lambda i, c: (0, 0, 0)
    return pl.pallas_call(
        grads_kernel,
        grid_spec=pltpu.PrefetchScalarGridSpec(
            num_scalar_prefetch=1,
            grid=(half // block,),
            in_specs=[
                pl.BlockSpec((rows, chan), step),
                pl.BlockSpec((rows, width), step),
                pl.BlockSpec((rows, width), step),
                pl.BlockSpec((block, cols, chan), line),
                pl.BlockSpec((block, cols, chan), line),
            ],
            out_specs=[
                pl.BlockSpec((chips, kept, chan), whole),
                pl.BlockSpec((chips, kept, chan), whole),
            ],
            scratch_shapes=[pltpu.VMEM((chan, width), F32), pltpu.VMEM((chan, width), F32)],
        ),
        out_shape=[
            jax.ShapeDtypeStruct((chips, kept, chan), F32),
            jax.ShapeDtypeStruct((chips, kept, chan), BF),
        ],
        compiler_params=pltpu.CompilerParams(vmem_limit_bytes=26 << 20),
        name="grads",
    )(core.reshape(1), in_hbm(hidden), in_hbm(d_pre), in_hbm(act), own, par)


def sum_kernel(recv_ref, out_ref):
    total = recv_ref[0].astype(F32)
    for t in range(1, recv_ref.shape[0]):
        total = total + recv_ref[t].astype(F32)
    out_ref[...] = total.astype(BF)


def sum_call(recv, rows):
    chips, _, chan = recv.shape
    return pl.pallas_call(
        sum_kernel,
        grid=(1,),
        in_specs=[pl.BlockSpec((chips, rows, chan), lambda i: (0, 0, 0))],
        out_specs=pl.BlockSpec((rows, chan), lambda i: (0, 0)),
        out_shape=jax.ShapeDtypeStruct((rows, chan), BF),
        compiler_params=pltpu.CompilerParams(vmem_limit_bytes=6 << 20),
        name="sum_parts",
    )(recv)


def mix_kernel(core_ref, u_ref, own_ref, par_ref, out_ref, re_ref, im_ref):
    even = core_ref[0] == 0
    own = own_ref[...].astype(F32)
    par = par_ref[...].astype(F32)
    first = jnp.where(even, own, par)
    second = jnp.where(even, par, own)
    chan = re_ref.shape[0]
    re_ref[...] = by_half(first, pltpu.roll(second, 4, 1)).reshape(chan, chan).astype(BF)
    im_ref[...] = by_half(pltpu.roll(first, 4, 1), second).reshape(chan, chan).astype(BF)
    half = u_ref.shape[0] // 2
    by_re = dot(u_ref[...], re_ref[...])
    by_im = dot(u_ref[...], im_ref[...])
    vr = by_re[:half] - by_im[half:]
    vi = by_re[half:] + by_im[:half]
    mixed = jnp.concatenate([vr, vi], axis=0).astype(BF)
    for t in range(out_ref.shape[0]):
        out_ref[t] = mixed


def mix_call(core, u, own, par):
    chips, _, chan = own.shape
    vmem = pl.BlockSpec(memory_space=pltpu.VMEM)
    return pl.pallas_call(
        mix_kernel,
        in_specs=[pl.BlockSpec(memory_space=pltpu.SMEM), vmem, vmem, vmem],
        out_specs=[vmem, vmem, vmem],
        out_shape=[
            pltpu.HBM((chips, u.shape[0], chan), BF),
            pltpu.HBM((chan, chan), BF),
            pltpu.HBM((chan, chan), BF),
        ],
        compiler_params=pltpu.CompilerParams(vmem_limit_bytes=8 << 20),
        name="mix",
    )(core.reshape(1), u, own, par)


def last_kernel(core_ref, u_ref, upar_ref, d_ref, dpar_ref, re_ref, im_ref, gown_ref, gpar_ref, out_ref, du_ref):
    even = core_ref[0] == 0
    both = d_ref.shape[0]
    half = both // 2
    chips, kept, chan = gown_ref.shape
    across = (((1,), (1,)), ((), ()))
    by_re = lax.dot_general(d_ref[...], re_ref[...], across, preferred_element_type=F32)
    by_im = lax.dot_general(d_ref[...], im_ref[...], across, preferred_element_type=F32)
    du_re = by_re[:half] + by_im[half:]
    du_im = by_re[half:] - by_im[:half]
    du = jnp.concatenate([du_re, du_im], axis=0).astype(BF)
    u_re = jnp.concatenate([u_ref[:half], upar_ref[:half]], axis=0)
    u_im = jnp.concatenate([u_ref[half:], upar_ref[half:]], axis=0)
    d_re = jnp.concatenate([d_ref[:half], dpar_ref[:half]], axis=0)
    d_im = jnp.concatenate([d_ref[half:], dpar_ref[half:]], axis=0)
    u_all = jnp.concatenate([u_re, u_im], axis=0)
    g_re = rows_dot(u_all, jnp.concatenate([d_re, d_im], axis=0)).reshape(chips, 8, chan)
    g_im = rows_dot(u_all, jnp.concatenate([d_im, -d_re], axis=0)).reshape(chips, 8, chan)
    low = jnp.where(even, g_re, pltpu.roll(g_re, 4, 1))
    high = jnp.where(even, pltpu.roll(g_im, 4, 1), g_im)
    out_ref[:, kept:, :] = by_half(low, high).astype(BF)
    for t in range(chips):
        du_ref[t] = du
        out_ref[t, :kept, :] = (gown_ref[t] + gpar_ref[t].astype(F32)).astype(BF)


def last_call(core, u, u_par, d, d_par, w_re, w_im, g_own, g_par):
    chips, kept, chan = g_own.shape
    vmem = pl.BlockSpec(memory_space=pltpu.VMEM)
    return pl.pallas_call(
        last_kernel,
        in_specs=[pl.BlockSpec(memory_space=pltpu.SMEM)] + [vmem] * 8,
        out_specs=[vmem, vmem],
        out_shape=[
            jax.ShapeDtypeStruct((chips, kept + 8, chan), BF),
            jax.ShapeDtypeStruct((chips, d.shape[0], chan), BF),
        ],
        compiler_params=pltpu.CompilerParams(vmem_limit_bytes=14 << 20),
        name="last",
    )(core.reshape(1), u, u_par, d, d_par, w_re, w_im, g_own, g_par)


def lines_kernel(recv_ref, out_ref):
    groups, _, _ = out_ref.shape
    chips, kept, _ = recv_ref.shape
    own = kept - 8
    total = recv_ref[0, :own, :].astype(F32)
    for t in range(1, chips):
        total = total + recv_ref[t, :own, :].astype(F32)
    per = chips // groups
    for g in range(groups):
        parts = [total[8 * g : 8 * g + 8]]
        parts += [recv_ref[t, own:, :].astype(F32) for t in range(g * per, (g + 1) * per)]
        out_ref[g] = jnp.concatenate(parts, axis=0).astype(BF)


def lines_call(recv, groups):
    chips, _, chan = recv.shape
    per = chips // groups
    vmem = pl.BlockSpec(memory_space=pltpu.VMEM)
    return pl.pallas_call(
        lines_kernel,
        in_specs=[vmem],
        out_specs=vmem,
        out_shape=jax.ShapeDtypeStruct((groups, 8 + 8 * per, chan), BF),
        compiler_params=pltpu.CompilerParams(vmem_limit_bytes=8 << 20),
        name="lines_rows",
    )(recv)


def final_kernel(own_ref, one_ref, two_ref, three_ref, mode_ref, in_ref, out_ref, *, scale_mlp, scale_mode):
    total = own_ref[...].astype(F32)
    for ref in (one_ref, two_ref, three_ref):
        total = total + ref[...].astype(F32)
    in_ref[...] = total[:4] * scale_mlp
    out_ref[...] = total[4:8] * scale_mlp
    for k in range(mode_ref.shape[1]):
        mode_ref[0, k] = total[8 * k + 8 : 8 * k + 12] * scale_mode
        mode_ref[1, k] = total[8 * k + 12 : 8 * k + 16] * scale_mode


def final_call(parts, scale_mlp, scale_mode):
    rows, chan = parts[0].shape
    vmem = pl.BlockSpec(memory_space=pltpu.VMEM)
    return pl.pallas_call(
        functools.partial(final_kernel, scale_mlp=scale_mlp, scale_mode=scale_mode),
        in_specs=[vmem] * 4,
        out_specs=[vmem] * 3,
        out_shape=[
            jax.ShapeDtypeStruct((2, rows // 8 - 1, 4, chan), F32),
            jax.ShapeDtypeStruct((4, chan), F32),
            jax.ShapeDtypeStruct((4, chan), F32),
        ],
        compiler_params=pltpu.CompilerParams(vmem_limit_bytes=4 << 20),
        name="final",
    )(*parts)


def own_kernel(gy_ref, blocks_ref, out_ref):
    out_ref[...] = blocks_ref[0]


def own_call(gy, blocks):
    _, rows, chan = blocks.shape
    return pl.pallas_call(
        own_kernel,
        grid_spec=pltpu.PrefetchScalarGridSpec(
            num_scalar_prefetch=1,
            grid=(1,),
            in_specs=[pl.BlockSpec((1, rows, chan), lambda i, g: (g[0], 0, 0))],
            out_specs=pl.BlockSpec((rows, chan), lambda i, g: (0, 0)),
        ),
        out_shape=jax.ShapeDtypeStruct((rows, chan), BF),
        compiler_params=pltpu.CompilerParams(vmem_limit_bytes=2 << 20),
        name="own_rows",
    )(gy.reshape(1), blocks)


def local(inputs, cotangent, mode_weight, w_in, w_out):
    lines, cols, chan = inputs.shape
    nx = lax.axis_size("gx")
    ny = lax.axis_size("gy")
    chips = nx // 2
    total_x = cols * nx
    half = lines // 2
    own_rows = chan // nx
    me = lax.axis_index("gx")
    gy = lax.axis_index("gy")
    core = me % 2
    groups = [[2 * t + c for t in range(chips)] for c in range(2)]
    swap = [(i, i ^ 1) for i in range(nx)]

    def pair(x):
        return lax.ppermute(x, "gx", swap)

    def spread(x):
        return lax.all_to_all(x, "gx", 0, 0, tiled=True, axis_index_groups=groups)

    def pick(x, which, axis):
        return lax.dynamic_index_in_dim(x, which, axis, keepdims=False)

    inp2 = inputs.reshape(2, half, cols, chan)
    cot2 = cotangent.reshape(2, half, cols, chan)
    in_par = pair(pick(inp2, 1 - core, 0))
    cot_par = pair(pick(cot2, 1 - core, 0))
    in_own = pick(inp2, core, 0)
    cot_own = pick(cot2, core, 0)
    steps = jnp.arange(cols, dtype=jnp.int32)
    own_fwd, own_inv = bases(me * cols + steps, total_x, M)
    par_fwd, par_inv = bases((me ^ 1) * cols + steps, total_x, M)
    inv = jnp.concatenate([own_inv, par_inv], axis=0)

    spec_part = contract("yxc,xm->myc", in_own, own_fwd) + contract("yxc,xm->myc", in_par, par_fwd)
    spec_part = spec_part.astype(BF).reshape(chips, 2 * half, chan)
    weight_rows = mode_weight.transpose(1, 0, 2, 3).reshape(M, 2 * own_rows, chan)
    recv = spread(jnp.concatenate([spec_part, weight_rows], axis=1))
    both = 2 * half
    w_mine = recv[:, both:]
    w_par = pair(w_mine)
    spec = sum_call(recv, both)
    sent, w_re, w_im = mix_call(core, spec, w_mine, w_par)
    mixed = spread(sent)
    spec_par = pair(spec)
    hidden, act, d_pre, d_part = mlp_call(
        mixed.reshape(2 * M * half, chan), cot_own, cot_par, inv, w_in, in_hbm(w_out.T)
    )
    dv = spread(d_part.reshape(chips, both, chan))
    g_own, g_send = grads_call(core, hidden, d_pre, act, cot_own, cot_par, chips)
    g_par = pair(g_send)
    dv = sum_call(dv, both)
    dv_par = pair(dv)
    sent, du = last_call(core, spec, spec_par, dv, dv_par, w_re, w_im, g_own, g_par)
    recv = spread(sent)
    recv, du = lax.optimization_barrier((recv, du))
    du_own = spread(du)
    du_par = pair(du_own)
    blocks = lines_call(recv, ny)
    scale_mlp = 1.0 / math.sqrt(lines * ny * total_x)
    scale_mode = 1.0 / math.sqrt(lines * ny)
    parts = [own_call(gy, blocks)]
    for d in range(1, ny):
        sent = pick(blocks, (gy + d) % ny, 0)
        parts.append(lax.ppermute(sent, "gy", [(i, (i + d) % ny) for i in range(ny)]))
    d_mode, tail_in, tail_out = final_call(parts, scale_mlp, scale_mode)

    du_lo = jnp.where(core == 0, du_own, du_par).reshape(2 * M, half, chan)
    du_hi = jnp.where(core == 0, du_par, du_own).reshape(2 * M, half, chan)
    ret_lo = contract("myc,xm->yxc", du_lo, own_fwd)
    ret_hi = contract("myc,xm->yxc", du_hi, own_fwd)
    returned = jnp.concatenate([ret_lo, ret_hi], axis=0)
    d_inputs = (cotangent.astype(F32) + returned).astype(BF)
    return (d_inputs, d_mode, tail_in.T, tail_out)


def solution(mesh):
    placed = (P("gy", "gx", None), P("gy", "gx", None), P(None, None, "gx", None), P(), P())
    return jax.shard_map(
        local,
        mesh=mesh,
        in_specs=placed,
        out_specs=(
            P("gy", "gx", None),
            P(None, "gy", "gx", None),
            P(None, ("gy", "gx")),
            P(("gy", "gx"), None),
        ),
        check_vma=False,
    )
```

```python
import functools
import math

import jax
import jax.numpy as jnp
from jax import lax
from jax.experimental import pallas as pl
from jax.experimental.pallas import tpu as pltpu
from jax.sharding import PartitionSpec as P

M = 32
LANES = 128
BF = jnp.bfloat16
F32 = jnp.float32


def bases(positions, length, modes):
    order = jnp.arange(modes, dtype=jnp.int32)
    phase = positions[:, None] * order[None, :] % length
    angle = phase.astype(F32) * (2.0 * math.pi / length)
    factor = 1.0 / math.sqrt(length)
    cosine = jnp.cos(angle) * factor
    sine = jnp.sin(angle) * factor
    weight = jnp.where(order == 0, 1.0, 2.0).astype(F32)
    forward = jnp.stack([cosine, -sine], axis=2).astype(BF)
    inverse = jnp.stack([cosine * weight, -sine * weight], axis=2).astype(BF)
    size = positions.shape[0]
    return forward.reshape(size, 2 * modes), inverse.reshape(size, 2 * modes)


def contract(form, left, right):
    return jnp.einsum(form, left, right, preferred_element_type=F32)


def dot(left, right):
    return jnp.dot(left, right, preferred_element_type=F32)


def rows_dot(left, right):
    return lax.dot_general(left, right, (((0,), (0,)), ((), ())), preferred_element_type=F32)


GELU_A = math.sqrt(2.0 / math.pi)
GELU_B = 0.044715 * GELU_A


def mlp_kernel(
    mix_ref, own_ref, par_ref, inv_ref, invt_ref, wi_ref, wit_ref, wot_ref,
    hid_ref, act_ref, dpre_ref, part_ref,
    mix_lo, mix_hi, part_lo, part_hi, pre_s, ga_s, dh_s,
):
    i = pl.program_id(0)
    block, cols, chan = own_ref.shape
    modes = inv_ref.shape[1]
    half = mix_ref.shape[0] // modes
    side = block * cols
    chunk = 32

    @pl.when(i == 0)
    def _():
        mix_lo[...] = mix_ref[:, :LANES].astype(F32)
        mix_hi[...] = mix_ref[:, LANES:].astype(F32)

    for b in range(block):
        lines = pl.ds(i * block + b, modes, stride=half)
        table = jnp.concatenate([mix_lo[lines, :], mix_hi[lines, :]], axis=1).astype(BF)
        h = dot(inv_ref[...], table).astype(BF)
        hid_ref[b * cols : (b + 1) * cols, :] = h[:cols]
        hid_ref[side + b * cols : side + (b + 1) * cols, :] = h[cols:]
    flat = (side, chan)
    cot = jnp.concatenate([own_ref[...].reshape(flat), par_ref[...].reshape(flat)], axis=0)
    pre_s[...] = dot(hid_ref[...], wi_ref[...])
    ga_s[...] = dot(cot, wot_ref[...])
    for r in range(0, 2 * side, chunk):
        p = pre_s[r : r + chunk, :]
        g = ga_s[r : r + chunk, :]
        sq = p * p
        t = 0.5 * jnp.tanh(p * (GELU_A + GELU_B * sq))
        s = 0.5 + t
        a = p * s
        slope = s + (a * (0.5 - t)) * (2.0 * GELU_A + (6.0 * GELU_B) * sq)
        act_ref[r : r + chunk, :] = a.astype(BF)
        dpre_ref[r : r + chunk, :] = (g * slope).astype(BF)
    dh_s[...] = dot(dpre_ref[...], wit_ref[...])
    for b in range(block):
        lines = pl.ds(i * block + b, modes, stride=half)
        mine = dh_s[b * cols : (b + 1) * cols, :]
        other = dh_s[side + b * cols : side + (b + 1) * cols, :]
        sums = dot(invt_ref[...], jnp.concatenate([mine, other], axis=0).astype(BF))
        part_lo[lines, :] = sums[:, :LANES]
        part_hi[lines, :] = sums[:, LANES:]

    @pl.when(i == pl.num_programs(0) - 1)
    def _():
        part_ref[:, :LANES] = part_lo[...].astype(BF)
        part_ref[:, LANES:] = part_hi[...].astype(BF)


def mlp_call(mix, own, par, inv, w_in, w_out_t, block=4):
    half, cols, chan = own.shape
    modes = inv.shape[1]
    width = w_in.shape[1]
    rows = 2 * block * cols
    whole = lambda i: (0, 0)
    step = lambda i: (i, 0)
    line = lambda i: (i, 0, 0)
    return pl.pallas_call(
        mlp_kernel,
        grid=(half // block,),
        in_specs=[
            pl.BlockSpec((modes * half, chan), whole),
            pl.BlockSpec((block, cols, chan), line),
            pl.BlockSpec((block, cols, chan), line),
            pl.BlockSpec((2 * cols, modes), whole),
            pl.BlockSpec((modes, 2 * cols), whole),
            pl.BlockSpec((chan, width), whole),
            pl.BlockSpec((width, chan), whole),
            pl.BlockSpec((chan, width), whole),
        ],
        out_specs=[
            pl.BlockSpec((rows, chan), step),
            pl.BlockSpec((rows, width), step),
            pl.BlockSpec((rows, width), step),
            pl.BlockSpec((modes * half, chan), whole),
        ],
        out_shape=[
            pltpu.HBM((2 * half * cols, chan), BF),
            pltpu.HBM((2 * half * cols, width), BF),
            pltpu.HBM((2 * half * cols, width), BF),
            pltpu.HBM((modes * half, chan), BF),
        ],
        scratch_shapes=[pltpu.VMEM((modes * half, LANES), F32)] * 4
        + [pltpu.VMEM((rows, width), F32)] * 2
        + [pltpu.VMEM((rows, chan), F32)],
        compiler_params=pltpu.CompilerParams(vmem_limit_bytes=30 << 20),
        name="mlp",
    )(mix, own, par, inv, inv.T, w_in, w_in.T, w_out_t)


def by_half(low, high):
    row = lax.broadcasted_iota(jnp.int32, low.shape, 1)
    return jnp.where(row < 4, low, high)


def grads_kernel(core_ref, hid_ref, dpre_ref, act_ref, own_ref, par_ref, keep_ref, send_ref, acc_in, acc_out):
    i = pl.program_id(0)
    block, cols, chan = own_ref.shape
    chips, kept, chan = keep_ref.shape
    groups = kept // 8

    @pl.when(i == 0)
    def _():
        acc_in[...] = jnp.zeros_like(acc_in)
        acc_out[...] = jnp.zeros_like(acc_out)

    acc_in[...] += rows_dot(hid_ref[...], dpre_ref[...])
    flat = (block * cols, own_ref.shape[2])
    cot = jnp.concatenate([own_ref[...].reshape(flat), par_ref[...].reshape(flat)], axis=0)
    acc_out[...] += rows_dot(cot, act_ref[...])

    @pl.when(i == pl.num_programs(0) - 1)
    def _():
        even = core_ref[0] == 0
        g_in = acc_in[...].T.reshape(groups * chips, 8, chan)
        g_out = acc_out[...].T.reshape(groups * chips, 8, chan)
        lows = by_half(g_in, pltpu.roll(g_out, 4, 1))
        highs = by_half(pltpu.roll(g_in, 4, 1), g_out)
        keep = jnp.where(even, lows, highs)
        send = jnp.where(even, highs, lows)
        for t in range(chips):
            keep_ref[t] = jnp.concatenate([keep[g * chips + t] for g in range(groups)], axis=0)
            send_ref[t] = jnp.concatenate([send[g * chips + t] for g in range(groups)], axis=0).astype(BF)


def in_hbm(x):
    return pltpu.with_memory_space_constraint(x, pltpu.HBM)


def grads_call(core, hidden, d_pre, act, own, par, chips, block=4):
    half, cols, chan = own.shape
    width = act.shape[1]
    rows = block * 2 * cols
    kept = width // chips
    step = lambda i, c: (i, 0)
    line = lambda i, c: (i, 0, 0)
    whole = lambda i, c: (0, 0, 0)
    return pl.pallas_call(
        grads_kernel,
        grid_spec=pltpu.PrefetchScalarGridSpec(
            num_scalar_prefetch=1,
            grid=(half // block,),
            in_specs=[
                pl.BlockSpec((rows, chan), step),
                pl.BlockSpec((rows, width), step),
                pl.BlockSpec((rows, width), step),
                pl.BlockSpec((block, cols, chan), line),
                pl.BlockSpec((block, cols, chan), line),
            ],
            out_specs=[
                pl.BlockSpec((chips, kept, chan), whole),
                pl.BlockSpec((chips, kept, chan), whole),
            ],
            scratch_shapes=[pltpu.VMEM((chan, width), F32), pltpu.VMEM((chan, width), F32)],
        ),
        out_shape=[
            jax.ShapeDtypeStruct((chips, kept, chan), F32),
            jax.ShapeDtypeStruct((chips, kept, chan), BF),
        ],
        compiler_params=pltpu.CompilerParams(vmem_limit_bytes=34 << 20),
        name="grads",
    )(core.reshape(1), in_hbm(hidden), in_hbm(d_pre), in_hbm(act), own, par)


def sum_kernel(recv_ref, out_ref):
    total = recv_ref[0].astype(F32)
    for t in range(1, recv_ref.shape[0]):
        total = total + recv_ref[t].astype(F32)
    out_ref[...] = total.astype(BF)


def sum_call(recv, rows):
    chips, _, chan = recv.shape
    return pl.pallas_call(
        sum_kernel,
        grid=(1,),
        in_specs=[pl.BlockSpec((chips, rows, chan), lambda i: (0, 0, 0))],
        out_specs=pl.BlockSpec((rows, chan), lambda i: (0, 0)),
        out_shape=jax.ShapeDtypeStruct((rows, chan), BF),
        compiler_params=pltpu.CompilerParams(vmem_limit_bytes=6 << 20),
        name="sum_parts",
    )(recv)


def mix_kernel(core_ref, u_ref, own_ref, par_ref, out_ref, re_ref, im_ref):
    even = core_ref[0] == 0
    own = own_ref[...].astype(F32)
    par = par_ref[...].astype(F32)
    first = jnp.where(even, own, par)
    second = jnp.where(even, par, own)
    chan = re_ref.shape[0]
    re_ref[...] = by_half(first, pltpu.roll(second, 4, 1)).reshape(chan, chan).astype(BF)
    im_ref[...] = by_half(pltpu.roll(first, 4, 1), second).reshape(chan, chan).astype(BF)
    half = u_ref.shape[0] // 2
    by_re = dot(u_ref[...], re_ref[...])
    by_im = dot(u_ref[...], im_ref[...])
    vr = by_re[:half] - by_im[half:]
    vi = by_re[half:] + by_im[:half]
    mixed = jnp.concatenate([vr, vi], axis=0).astype(BF)
    for t in range(out_ref.shape[0]):
        out_ref[t] = mixed


def mix_call(core, u, own, par):
    chips, _, chan = own.shape
    vmem = pl.BlockSpec(memory_space=pltpu.VMEM)
    return pl.pallas_call(
        mix_kernel,
        in_specs=[pl.BlockSpec(memory_space=pltpu.SMEM), vmem, vmem, vmem],
        out_specs=[vmem, vmem, vmem],
        out_shape=[
            pltpu.HBM((chips, u.shape[0], chan), BF),
            pltpu.HBM((chan, chan), BF),
            pltpu.HBM((chan, chan), BF),
        ],
        compiler_params=pltpu.CompilerParams(vmem_limit_bytes=8 << 20),
        name="mix",
    )(core.reshape(1), u, own, par)


def last_kernel(core_ref, u_ref, upar_ref, d_ref, dpar_ref, re_ref, im_ref, gown_ref, gpar_ref, out_ref, du_ref):
    even = core_ref[0] == 0
    both = d_ref.shape[0]
    half = both // 2
    chips, kept, chan = gown_ref.shape
    across = (((1,), (1,)), ((), ()))
    by_re = lax.dot_general(d_ref[...], re_ref[...], across, preferred_element_type=F32)
    by_im = lax.dot_general(d_ref[...], im_ref[...], across, preferred_element_type=F32)
    du_re = by_re[:half] + by_im[half:]
    du_im = by_re[half:] - by_im[:half]
    du = jnp.concatenate([du_re, du_im], axis=0).astype(BF)
    u_re = jnp.concatenate([u_ref[:half], upar_ref[:half]], axis=0)
    u_im = jnp.concatenate([u_ref[half:], upar_ref[half:]], axis=0)
    d_re = jnp.concatenate([d_ref[:half], dpar_ref[:half]], axis=0)
    d_im = jnp.concatenate([d_ref[half:], dpar_ref[half:]], axis=0)
    u_all = jnp.concatenate([u_re, u_im], axis=0)
    g_re = rows_dot(u_all, jnp.concatenate([d_re, d_im], axis=0)).reshape(chips, 8, chan)
    g_im = rows_dot(u_all, jnp.concatenate([d_im, -d_re], axis=0)).reshape(chips, 8, chan)
    low = jnp.where(even, g_re, pltpu.roll(g_re, 4, 1))
    high = jnp.where(even, pltpu.roll(g_im, 4, 1), g_im)
    out_ref[:, kept:, :] = by_half(low, high).astype(BF)
    for t in range(chips):
        du_ref[t] = du
        out_ref[t, :kept, :] = (gown_ref[t] + gpar_ref[t].astype(F32)).astype(BF)


def last_call(core, u, u_par, d, d_par, w_re, w_im, g_own, g_par):
    chips, kept, chan = g_own.shape
    vmem = pl.BlockSpec(memory_space=pltpu.VMEM)
    return pl.pallas_call(
        last_kernel,
        in_specs=[pl.BlockSpec(memory_space=pltpu.SMEM)] + [vmem] * 8,
        out_specs=[vmem, vmem],
        out_shape=[
            jax.ShapeDtypeStruct((chips, kept + 8, chan), BF),
            jax.ShapeDtypeStruct((chips, d.shape[0], chan), BF),
        ],
        compiler_params=pltpu.CompilerParams(vmem_limit_bytes=14 << 20),
        name="last",
    )(core.reshape(1), u, u_par, d, d_par, w_re, w_im, g_own, g_par)


def lines_kernel(recv_ref, out_ref):
    groups, _, _ = out_ref.shape
    chips, kept, _ = recv_ref.shape
    own = kept - 8
    total = recv_ref[0, :own, :].astype(F32)
    for t in range(1, chips):
        total = total + recv_ref[t, :own, :].astype(F32)
    per = chips // groups
    for g in range(groups):
        parts = [total[8 * g : 8 * g + 8]]
        parts += [recv_ref[t, own:, :].astype(F32) for t in range(g * per, (g + 1) * per)]
        out_ref[g] = jnp.concatenate(parts, axis=0).astype(BF)


def lines_call(recv, groups):
    chips, _, chan = recv.shape
    per = chips // groups
    vmem = pl.BlockSpec(memory_space=pltpu.VMEM)
    return pl.pallas_call(
        lines_kernel,
        in_specs=[vmem],
        out_specs=vmem,
        out_shape=jax.ShapeDtypeStruct((groups, 8 + 8 * per, chan), BF),
        compiler_params=pltpu.CompilerParams(vmem_limit_bytes=8 << 20),
        name="lines_rows",
    )(recv)


def final_kernel(own_ref, one_ref, two_ref, three_ref, mode_ref, in_ref, out_ref, *, scale_mlp, scale_mode):
    total = own_ref[...].astype(F32)
    for ref in (one_ref, two_ref, three_ref):
        total = total + ref[...].astype(F32)
    in_ref[...] = total[:4] * scale_mlp
    out_ref[...] = total[4:8] * scale_mlp
    for k in range(mode_ref.shape[1]):
        mode_ref[0, k] = total[8 * k + 8 : 8 * k + 12] * scale_mode
        mode_ref[1, k] = total[8 * k + 12 : 8 * k + 16] * scale_mode


def final_call(parts, scale_mlp, scale_mode):
    rows, chan = parts[0].shape
    vmem = pl.BlockSpec(memory_space=pltpu.VMEM)
    return pl.pallas_call(
        functools.partial(final_kernel, scale_mlp=scale_mlp, scale_mode=scale_mode),
        in_specs=[vmem] * 4,
        out_specs=[vmem] * 3,
        out_shape=[
            jax.ShapeDtypeStruct((2, rows // 8 - 1, 4, chan), F32),
            jax.ShapeDtypeStruct((4, chan), F32),
            jax.ShapeDtypeStruct((4, chan), F32),
        ],
        compiler_params=pltpu.CompilerParams(vmem_limit_bytes=4 << 20),
        name="final",
    )(*parts)


def own_kernel(gy_ref, blocks_ref, out_ref):
    out_ref[...] = blocks_ref[0]


def own_call(gy, blocks):
    _, rows, chan = blocks.shape
    return pl.pallas_call(
        own_kernel,
        grid_spec=pltpu.PrefetchScalarGridSpec(
            num_scalar_prefetch=1,
            grid=(1,),
            in_specs=[pl.BlockSpec((1, rows, chan), lambda i, g: (g[0], 0, 0))],
            out_specs=pl.BlockSpec((rows, chan), lambda i, g: (0, 0)),
        ),
        out_shape=jax.ShapeDtypeStruct((rows, chan), BF),
        compiler_params=pltpu.CompilerParams(vmem_limit_bytes=2 << 20),
        name="own_rows",
    )(gy.reshape(1), blocks)


def local(inputs, cotangent, mode_weight, w_in, w_out):
    lines, cols, chan = inputs.shape
    nx = lax.axis_size("gx")
    ny = lax.axis_size("gy")
    chips = nx // 2
    total_x = cols * nx
    half = lines // 2
    own_rows = chan // nx
    me = lax.axis_index("gx")
    gy = lax.axis_index("gy")
    core = me % 2
    groups = [[2 * t + c for t in range(chips)] for c in range(2)]
    swap = [(i, i ^ 1) for i in range(nx)]

    def pair(x):
        return lax.ppermute(x, "gx", swap)

    def spread(x):
        return lax.all_to_all(x, "gx", 0, 0, tiled=True, axis_index_groups=groups)

    def pick(x, which, axis):
        return lax.dynamic_index_in_dim(x, which, axis, keepdims=False)

    inp2 = inputs.reshape(2, half, cols, chan)
    cot2 = cotangent.reshape(2, half, cols, chan)
    in_par = pair(pick(inp2, 1 - core, 0))
    cot_par = pair(pick(cot2, 1 - core, 0))
    in_own = pick(inp2, core, 0)
    cot_own = pick(cot2, core, 0)
    steps = jnp.arange(cols, dtype=jnp.int32)
    own_fwd, own_inv = bases(me * cols + steps, total_x, M)
    par_fwd, par_inv = bases((me ^ 1) * cols + steps, total_x, M)
    inv = jnp.concatenate([own_inv, par_inv], axis=0)

    spec_part = contract("yxc,xm->myc", in_own, own_fwd) + contract("yxc,xm->myc", in_par, par_fwd)
    spec_part = spec_part.astype(BF).reshape(chips, 2 * half, chan)
    weight_rows = mode_weight.transpose(1, 0, 2, 3).reshape(M, 2 * own_rows, chan)
    recv = spread(jnp.concatenate([spec_part, weight_rows], axis=1))
    both = 2 * half
    w_mine = recv[:, both:]
    w_par = pair(w_mine)
    spec = sum_call(recv, both)
    sent, w_re, w_im = mix_call(core, spec, w_mine, w_par)
    mixed = spread(sent)
    spec_par = pair(spec)
    hidden, act, d_pre, d_part = mlp_call(
        mixed.reshape(2 * M * half, chan), cot_own, cot_par, inv, w_in, in_hbm(w_out.T)
    )
    dv = spread(d_part.reshape(chips, both, chan))
    g_own, g_send = grads_call(core, hidden, d_pre, act, cot_own, cot_par, chips)
    g_par = pair(g_send)
    dv = sum_call(dv, both)
    dv_par = pair(dv)
    sent, du = last_call(core, spec, spec_par, dv, dv_par, w_re, w_im, g_own, g_par)
    recv = spread(sent)
    recv, du = lax.optimization_barrier((recv, du))
    du_own = spread(du)
    du_par = pair(du_own)
    blocks = lines_call(recv, ny)
    scale_mlp = 1.0 / math.sqrt(lines * ny * total_x)
    scale_mode = 1.0 / math.sqrt(lines * ny)
    parts = [own_call(gy, blocks)]
    for d in range(1, ny):
        sent = pick(blocks, (gy + d) % ny, 0)
        parts.append(lax.ppermute(sent, "gy", [(i, (i + d) % ny) for i in range(ny)]))
    d_mode, tail_in, tail_out = final_call(parts, scale_mlp, scale_mode)

    du_lo = jnp.where(core == 0, du_own, du_par).reshape(2 * M, half, chan)
    du_hi = jnp.where(core == 0, du_par, du_own).reshape(2 * M, half, chan)
    ret_lo = contract("myc,xm->yxc", du_lo, own_fwd)
    ret_hi = contract("myc,xm->yxc", du_hi, own_fwd)
    returned = jnp.concatenate([ret_lo, ret_hi], axis=0)
    d_inputs = (cotangent.astype(F32) + returned).astype(BF)
    return (d_inputs, d_mode, tail_in.T, tail_out)


def solution(mesh):
    placed = (P("gy", "gx", None), P("gy", "gx", None), P(None, None, "gx", None), P(), P())
    return jax.shard_map(
        local,
        mesh=mesh,
        in_specs=placed,
        out_specs=(
            P("gy", "gx", None),
            P(None, "gy", "gx", None),
            P(None, ("gy", "gx")),
            P(("gy", "gx"), None),
        ),
        check_vma=False,
    )
```
